32 devices in a mesh: region: 4 (over y, x), cluster: 8 (over z, core).
Axes of the slice: x: 2, y: 2, z: 4, core: 2. Of those that a mesh axis runs over, the one named last changes fastest.
Arguments:
- pilots: bfloat16 [128, 1024, 1024], P(('region', 'cluster')), may hold values from -0.1875 to 0.1875
- estimate: bfloat16 [128, 8, 1024], P(('region', 'cluster')), may hold values from -6 to 6
- visible: int32 [128, 1024], P(('region', 'cluster')), may hold values from 0 to 65535, as said below
- blocks: int32 [128], P(('region', 'cluster')), may hold values from 4 to 8
- received: float32 [128, 8, 1024], P(('region', 'cluster')), may hold values from -6 to 6
- previous: float32 [128, 8, 1024], P(('region', 'cluster')), may hold values from -6 to 6
- onsager: float32 [128], P(('region', 'cluster')), may hold values from 0.2 to 0.8
- user_cluster: int32 [65536], replicated, may hold values from 0 to 15
- cluster_prior: float32 [16], replicated, may hold values from -4 to 0
Outputs:
- new_estimate: bfloat16 [128, 8, 1024], P(('region', 'cluster'))
- residual: float32 [128, 8, 1024], P(('region', 'cluster'))
- posterior: float32 [65536], P(('region', 'cluster'))
The draws below stay inside these ranges and needn't reach their ends.
Inputs may be any that keep to these rules, and one draw needn't show every extreme that they name: Every draw has some access point with 8 live blocks. `visible`: users are numbered region by region, 2048 * 8 to a region, in the order of the devices along region+cluster. An access point hears only users of its own region or of the two regions beside it along region (the first and the last region are beside each other); most of the users it hears are of its own region.
All inputs are finite; a program needn't handle non-finite values.
Results may differ from the reference program's by a relative error of at most 0.0056.
Values sent between devices are 32-bit elements; how exact they have to be, the bound alone decides.
A program may use at most 192 MiB of HBM per device.

```python
import jax
import jax.numpy as jnp
from jax import lax

M = 8
L = 1024
ROW_BLOCK = 128
NB = 8
AP_DEV = 4
USER_CLUSTERS = 16
ROWS_AP = 1024
APS = 128
USERS = 65536
N_REGION = 4
N_CLUSTER = 8


def draw_visible(key, part):
    first, second = jax.random.split(jax.random.fold_in(key, 17))
    region_users = USERS // N_REGION
    home = jnp.arange(APS, dtype=jnp.int32) // AP_DEV // N_CLUSTER
    pick = jax.random.randint(first, (APS, ROWS_AP), 0, 20, dtype=jnp.int32)
    offset = jnp.where(pick == 0, -1, jnp.where(pick == 1, 1, 0)).astype(jnp.int32)
    region = (home[:, None] + offset + N_REGION) % N_REGION
    inside = jax.random.randint(second, (APS, ROWS_AP), 0, region_users, dtype=jnp.int32)
    return (region * region_users + inside).astype(jnp.int32)


def plant(drawn, key, least, top_value):
    spot = [jax.random.randint(jax.random.fold_in(key, axis), (), 0, length) for axis, length in enumerate(drawn.shape)]
    longest = drawn.shape.index(max(drawn.shape))
    neighbour = spot[:longest] + [(spot[longest] + 1) % drawn.shape[longest]] + spot[longest + 1:]
    return drawn.at[tuple(spot)].set(least).at[tuple(neighbour)].set(top_value)


def level_of(key, dims, shards, smallest, largest):
    factor_of = 1.0
    for dim, blocks in shards:
        heights = jax.random.uniform(jax.random.fold_in(jax.random.fold_in(key, 6), dim), (blocks,), jnp.float32, smallest / len(shards), largest / len(shards))
        factor_of = factor_of * jnp.repeat(jnp.exp(heights), dims[dim] // blocks).reshape((-1,) + (1,) * (len(dims) - 1 - dim))
    return factor_of


def bell_draw(key, dims, scale, bound, cuts=(), kind=jnp.bfloat16):
    level = level_of(key, dims, cuts, -0.22, 0.18) if cuts else 1.0
    values = jax.random.normal(key, dims, jnp.float32) * scale * level
    return jnp.minimum(jnp.maximum(values, -bound), bound).astype(kind)


def setup_inputs(seed: int = 0) -> dict:
    keys = jax.random.split(jax.random.key(seed), 10)
    pilots = bell_draw(keys[0], (APS, ROWS_AP, L), L ** -0.5, 0.1875, ((0, 32),))
    estimate = bell_draw(keys[1], (APS, M, ROWS_AP), 0.7, 6.0, ((0, 32),))
    visible = draw_visible(jax.random.fold_in(keys[9], 71), 0)
    blocks = plant(jax.random.randint(keys[3], (APS,), NB // 2, NB + 1), jax.random.fold_in(keys[3], 1), NB // 2, NB).astype(jnp.int32)
    received = bell_draw(keys[4], (APS, M, L), 1.0, 6.0, ((0, 32),), jnp.float32)
    previous = bell_draw(keys[5], (APS, M, L), 1.0, 6.0, ((0, 32),), jnp.float32)
    onsager = jnp.clip(0.2 + 0.6 * jax.random.uniform(keys[6], (APS,), jnp.float32) ** level_of(keys[6], (APS,), ((0, 32),), -0.2, 0.2), 0.2, 0.8)
    user_cluster = plant(jax.random.randint(keys[7], (USERS,), 0, USER_CLUSTERS), jax.random.fold_in(keys[7], 1), 0, USER_CLUSTERS - 1).astype(jnp.int32)
    cluster_prior = jnp.clip(jax.random.uniform(keys[8], (USER_CLUSTERS,), jnp.float32, -4.0, 0.0), -4.0, 0.0)
    return {"pilots": pilots, "estimate": estimate, "visible": visible, "blocks": blocks, "received": received, "previous": previous, "onsager": onsager, "user_cluster": user_cluster, "cluster_prior": cluster_prior}


epsilon = 1e-6


def reference(pilots, estimate, visible, blocks, received, previous, onsager, user_cluster, cluster_prior):
    live = (jnp.arange(ROWS_AP)[None, :] // ROW_BLOCK) < blocks[:, None]
    masked = jnp.where(live[:, None, :], estimate, jnp.zeros_like(estimate))

    def per_point(items):
        pil, est, sig, prev, coef = items
        product = jnp.dot(est, pil, preferred_element_type=jnp.float32)
        resid = sig - product + coef * prev
        spread = jnp.mean(resid * resid) + epsilon
        narrow = resid.astype(jnp.bfloat16)
        stat = est.astype(jnp.float32) + jnp.dot(narrow, pil.T, preferred_element_type=jnp.float32)
        return resid, stat, spread

    resid, stat, spread = lax.map(per_point, (pilots, masked, received, previous, onsager))
    energy = jnp.sum(stat * stat, axis=1)
    base = 0.5 * M * jnp.log(spread / (1.0 + spread))
    llr = base[:, None] + energy / (2.0 * spread * (1.0 + spread))[:, None]
    llr = jnp.where(live, llr, jnp.float32(0.0))
    combined = jax.ops.segment_sum(llr.reshape(-1), visible.reshape(-1), num_segments=USERS)
    posterior = jax.nn.sigmoid(combined + cluster_prior[user_cluster])
    rate = posterior[visible]
    fresh = rate[:, None, :] * stat / (1.0 + spread)[:, None, None]
    new_estimate = jnp.where(live[:, None, :], fresh, jnp.float32(0.0)).astype(jnp.bfloat16)
    return new_estimate, resid, posterior
```

```python
import functools

import jax
import jax.numpy as jnp
from jax import lax
from jax.experimental import pallas as pl
from jax.experimental.pallas import tpu as pltpu
from jax.sharding import PartitionSpec as P

ROW_BLOCK = 128
LANES = 128
TILE = 384
VMEM_LIMIT = 48 * 1024 * 1024
MESH = pl.DeviceIdType.MESH

epsilon = 1e-06


def halves(value):
    high = value.astype(jnp.bfloat16)
    low = (value - high.astype(jnp.float32)).astype(jnp.bfloat16)
    return high, low


def relative_ids(visible, users):
    regions = lax.axis_size("region")
    lowest = lax.rem(lax.axis_index("region") + (regions - 1), regions) * (users // regions)
    shifted = visible - lowest
    shifted = jnp.where(shifted < 0, shifted + users, shifted)
    return shifted // LANES, shifted % LANES


def one_hot(row, count, start=0):
    place = lax.broadcasted_iota(jnp.int32, (count, row.shape[1]), 0) + start
    return place == row


def statistics_kernel(
    users, blocks_ref, onsager_ref, pilots_ref, estimate_ref, visible_ref, received_ref,
    previous_ref, resid_ref, scaled_ref, window_ref,
):
    point = pl.program_id(0)
    antennas, slots = estimate_ref.shape[1:]
    slot = lax.broadcasted_iota(jnp.int32, (1, slots), 1)
    live = slot // ROW_BLOCK < blocks_ref[point]
    widened = jnp.where(live, estimate_ref[0].astype(jnp.float32), 0.0)
    masked = widened.astype(jnp.bfloat16)
    pilots = pilots_ref[0]
    product = jnp.dot(masked, pilots, preferred_element_type=jnp.float32)
    resid = received_ref[0] - product + onsager_ref[point] * previous_ref[0]
    resid_ref[0] = resid
    square = jnp.sum(jnp.sum(resid * resid, axis=0, keepdims=True), axis=1, keepdims=True)
    spread = square / (antennas * resid.shape[1]) + epsilon
    narrow = resid.astype(jnp.bfloat16)
    stat = widened + lax.dot_general(
        narrow, pilots, (((1,), (1,)), ((), ())), preferred_element_type=jnp.float32
    )
    energy = jnp.sum(stat * stat, axis=0, keepdims=True)
    base = 0.5 * antennas * jnp.log(spread / (1.0 + spread))
    llr = jnp.where(live, base + energy / (2.0 * spread * (1.0 + spread)), 0.0)
    scaled_ref[0] = jnp.where(live, stat / (1.0 + spread), 0.0)
    high_id, low_id = relative_ids(visible_ref[pl.ds(point, 1), :], users)
    high, low = halves(llr)
    lanes = one_hot(low_id, LANES)
    spread_out = jnp.concatenate(
        [
            jnp.where(lanes, high.astype(jnp.float32), 0.0).astype(jnp.bfloat16),
            jnp.where(lanes, low.astype(jnp.float32), 0.0).astype(jnp.bfloat16),
        ],
        axis=0,
    )
    for start in range(0, window_ref.shape[0], TILE):
        rows = jnp.where(one_hot(high_id, TILE, start), 1.0, 0.0).astype(jnp.bfloat16)
        both = lax.dot_general(
            rows, spread_out, (((1,), (1,)), ((), ())), preferred_element_type=jnp.float32
        )
        part = both[:, :LANES] + both[:, LANES:]

        @pl.when(point == 0)
        def _():
            window_ref[pl.ds(start, TILE), :] = part

        @pl.when(point > 0)
        def _():
            window_ref[pl.ds(start, TILE), :] += part


def exchange_kernel(
    window_ref, labels_ref, prior_ref, owned_ref, nearby_ref, arrived, labels, label_sem,
    sum_send, sum_recv, post_send, post_recv,
):
    regions, clusters = lax.axis_size("region"), lax.axis_size("cluster")
    region, cluster = lax.axis_index("region"), lax.axis_index("cluster")
    rows = owned_ref.shape[0]
    peers = 3 * clusters
    home = clusters + cluster

    def peer(j):
        slot = lax.rem(home + j, peers)
        step = slot // clusters
        device = (lax.rem(region + step + (regions - 1), regions), lax.rem(slot, clusters))
        back = (2 - step) * clusters + cluster
        return slot, back, device

    def part(ref, slot):
        return ref.at[pl.ds(pl.multiple_of(slot * rows, rows), rows), :]

    def sum_copy(source, target, device):
        return pltpu.make_async_remote_copy(
            src_ref=part(window_ref, source), dst_ref=part(arrived, target),
            send_sem=sum_send.at[source], recv_sem=sum_recv.at[target],
            device_id=device, device_id_type=MESH,
        )

    def post_copy(source, target, device):
        return pltpu.make_async_remote_copy(
            src_ref=owned_ref, dst_ref=part(nearby_ref, target),
            send_sem=post_send.at[source], recv_sem=post_recv.at[target],
            device_id=device, device_id_type=MESH,
        )

    own_rows = pl.ds(pl.multiple_of((region * clusters + cluster) * rows, rows), rows)
    fetch = pltpu.make_async_copy(labels_ref.at[own_rows, :], labels, label_sem)
    fetch.start()
    barrier = pltpu.get_barrier_semaphore()

    @pl.loop(1, peers)
    def _(j):
        _, _, device = peer(j)
        pl.semaphore_signal(barrier, inc=1, device_id=device, device_id_type=MESH)

    pl.semaphore_wait(barrier, peers - 1)

    @pl.loop(1, peers)
    def _(j):
        slot, back, device = peer(j)
        sum_copy(slot, back, device).start()

    fetch.wait()
    total = jnp.zeros(owned_ref.shape, jnp.float32)
    for k in range(prior_ref.shape[0]):
        total = total + jnp.where(labels[...] == k, prior_ref[k], 0.0)
    total = total + window_ref[pl.ds(pl.multiple_of(home * rows, rows), rows), :]

    def collect(j, total):
        slot, back, device = peer(j)
        sum_copy(slot, slot, device).wait_recv()
        return total + arrived[pl.ds(pl.multiple_of(slot * rows, rows), rows), :]

    total = lax.fori_loop(1, peers, collect, total)
    posterior = jax.nn.sigmoid(total)
    owned_ref[...] = posterior
    nearby_ref[pl.ds(pl.multiple_of(home * rows, rows), rows), :] = posterior

    @pl.loop(1, peers)
    def _(j):
        slot, back, device = peer(j)
        post_copy(slot, back, device).start()

    @pl.loop(1, peers)
    def _(j):
        slot, back, device = peer(j)
        post_copy(slot, slot, device).wait_recv()

    @pl.loop(1, peers)
    def _(j):
        slot, back, device = peer(j)
        sum_copy(slot, back, device).wait_send()
        post_copy(slot, back, device).wait_send()


def denoise_kernel(users, visible_ref, scaled_ref, nearby_ref, fresh_ref):
    table = jnp.concatenate(halves(nearby_ref[...]), axis=1)
    for point in range(visible_ref.shape[0]):
        high_id, low_id = relative_ids(visible_ref[pl.ds(point, 1), :], users)
        picked = None
        for start in range(0, nearby_ref.shape[0], TILE):
            rows = jnp.where(one_hot(high_id, TILE, start), 1.0, 0.0).astype(jnp.bfloat16)
            term = lax.dot_general(
                table[start : start + TILE], rows, (((0,), (0,)), ((), ())),
                preferred_element_type=jnp.float32,
            )
            picked = term if picked is None else picked + term
        picked = picked[:LANES] + picked[LANES:]
        rate = jnp.sum(jnp.where(one_hot(low_id, LANES), picked, 0.0), axis=0, keepdims=True)
        fresh_ref[point] = (rate * scaled_ref[point]).astype(jnp.bfloat16)


def local(
    pilots, estimate, visible, blocks, received, previous, onsager, user_cluster, cluster_prior
):
    points, antennas, slots = estimate.shape
    length = pilots.shape[2]
    users = user_cluster.shape[0]
    regions, clusters = lax.axis_size("region"), lax.axis_size("cluster")
    rows = users // (regions * clusters) // LANES
    window_rows = 3 * clusters * rows
    f32 = jnp.float32
    smem = pl.BlockSpec(memory_space=pltpu.SMEM)
    vmem = pl.BlockSpec(memory_space=pltpu.VMEM)
    each = lambda *shape: pl.BlockSpec((1,) + shape, lambda i: (i, 0, 0))
    whole = lambda *shape: pl.BlockSpec(shape, lambda i: (0, 0))
    resid, scaled, window = pl.pallas_call(
        functools.partial(statistics_kernel, users),
        grid=(points,),
        in_specs=[
            smem, smem, each(slots, length), each(antennas, slots), whole(points, slots),
            each(antennas, length), each(antennas, length),
        ],
        out_specs=[each(antennas, length), each(antennas, slots), whole(window_rows, LANES)],
        out_shape=[
            jax.ShapeDtypeStruct((points, antennas, length), f32),
            jax.ShapeDtypeStruct((points, antennas, slots), f32),
            jax.ShapeDtypeStruct((window_rows, LANES), f32),
        ],
        compiler_params=pltpu.CompilerParams(vmem_limit_bytes=VMEM_LIMIT),
    )(blocks, onsager, pilots, estimate, visible, received, previous)
    peers = 3 * clusters
    owned, nearby = pl.pallas_call(
        exchange_kernel,
        in_specs=[vmem, pl.BlockSpec(memory_space=pl.ANY), smem],
        out_specs=[vmem, vmem],
        out_shape=[
            jax.ShapeDtypeStruct((rows, LANES), f32),
            jax.ShapeDtypeStruct((window_rows, LANES), f32),
        ],
        scratch_shapes=[
            pltpu.VMEM((window_rows, LANES), f32),
            pltpu.VMEM((rows, LANES), jnp.int32),
            pltpu.SemaphoreType.DMA,
        ]
        + [pltpu.SemaphoreType.DMA((peers,))] * 4,
        compiler_params=pltpu.CompilerParams(collective_id=0, has_side_effects=True),
    )(window, user_cluster.reshape(-1, LANES), cluster_prior)
    new_estimate = pl.pallas_call(
        functools.partial(denoise_kernel, users),
        in_specs=[vmem, vmem, vmem],
        out_specs=vmem,
        out_shape=jax.ShapeDtypeStruct((points, antennas, slots), jnp.bfloat16),
        compiler_params=pltpu.CompilerParams(vmem_limit_bytes=VMEM_LIMIT),
    )(visible, scaled, nearby)
    return (new_estimate, resid, owned.reshape(-1))


def solution(mesh):
    device = ("region", "cluster")
    placed = (
        P(device, None, None),
        P(device, None, None),
        P(device, None),
        P(device),
        P(device, None, None),
        P(device, None, None),
        P(device),
        P(),
        P(),
    )
    return jax.shard_map(
        local,
        mesh=mesh,
        in_specs=placed,
        out_specs=(P(device, None, None), P(device, None, None), P(device)),
        check_vma=False,
    )
```

```python
import functools

import jax
import jax.numpy as jnp
from jax import lax
from jax.experimental import pallas as pl
from jax.experimental.pallas import tpu as pltpu
from jax.sharding import PartitionSpec as P

ROW_BLOCK = 128
LANES = 128
TILE = 384
VMEM_LIMIT = 60 * 1024 * 1024
MESH = pl.DeviceIdType.MESH

epsilon = 1e-06


def halves(value):
    high = value.astype(jnp.bfloat16)
    low = (value - high.astype(jnp.float32)).astype(jnp.bfloat16)
    return high, low


def window_places(visible, users, rows):
    regions, clusters = lax.axis_size("region"), lax.axis_size("cluster")
    lowest = lax.rem(lax.axis_index("region") + (regions - 1), regions) * (users // regions)
    shifted = visible - lowest
    shifted = jnp.where(shifted < 0, shifted + users, shifted)
    line = lax.div(shifted, LANES)
    device = lax.div(line, rows)
    place = lax.rem(device, 2) * (3 * clusters // 2) + lax.div(device, 2)
    return place * rows + lax.rem(line, rows), lax.rem(shifted, LANES)


def one_hot(row, count, start=0):
    place = lax.broadcasted_iota(jnp.int32, (count, row.shape[1]), 0) + start
    return place == row


def main_kernel(
    pilots_hbm, estimate_hbm, visible_hbm, blocks_hbm, received_hbm, previous_hbm, onsager_hbm,
    labels_hbm, prior_hbm,
    resid_hbm, scaled_hbm, nearby_hbm,
    pilots, estimate, visible, blocks, received, previous, onsager, labels, prior,
    resid_out, scaled, nearby, selector, window, swapped, half, arrived, owned,
    load_sem, pilot_sem, store_sem, swap_sem, sum_send, sum_recv, post_send, post_recv,
):
    regions, clusters = lax.axis_size("region"), lax.axis_size("cluster")
    region, cluster = lax.axis_index("region"), lax.axis_index("cluster")
    core, chip, chips = lax.rem(cluster, 2), lax.div(cluster, 2), clusters // 2
    points, antennas, slots = estimate.shape
    rows = owned.shape[0]
    users = labels_hbm.shape[0] * LANES
    peers = 3 * chips
    half_rows = peers * rows
    home = chips + chip
    partner = (region, cluster + 1 - 2 * core)

    def part(ref, slot):
        return ref.at[pl.ds(pl.multiple_of(slot * rows, rows), rows), :]

    def side(ref, which):
        return ref.at[pl.ds(pl.multiple_of(which * half_rows, half_rows), half_rows), :]

    own_rows = pl.ds(pl.multiple_of((region * clusters + cluster) * rows, rows), rows)
    loads = [
        pltpu.make_async_copy(source, target, load_sem.at[i])
        for i, (source, target) in enumerate(
            [
                (visible_hbm, visible), (blocks_hbm, blocks), (estimate_hbm, estimate),
                (onsager_hbm, onsager), (received_hbm, received), (previous_hbm, previous),
                (prior_hbm, prior), (labels_hbm.at[own_rows, :], labels),
            ]
        )
    ]
    fetches = [
        pltpu.make_async_copy(pilots_hbm.at[i], pilots.at[i], pilot_sem.at[i])
        for i in range(points)
    ]
    for copy in loads[:4]:
        copy.start()
    fetches[0].start()
    for copy in loads[4:]:
        copy.start()
    for copy in fetches[1:]:
        copy.start()

    def peer(j):
        slot = lax.rem(home + j, peers)
        step = slot // chips
        device = (
            lax.rem(region + step + (regions - 1), regions), lax.rem(slot, chips) * 2 + core
        )
        back = (2 - step) * chips + chip
        return slot, back, device

    barrier = pltpu.get_barrier_semaphore()
    pl.semaphore_signal(barrier, inc=1, device_id=partner, device_id_type=MESH)

    @pl.loop(1, peers)
    def _(j):
        _, _, device = peer(j)
        pl.semaphore_signal(barrier, inc=1, device_id=device, device_id_type=MESH)

    loads[0].wait()
    row_id, lane_id = window_places(visible[...], users, rows)
    for point in range(points):
        for start in range(0, 2 * half_rows, TILE):
            selector[pl.ds(start, TILE), pl.ds(point * slots, slots)] = jnp.where(
                one_hot(row_id[point : point + 1], TILE, start), 1.0, 0.0
            ).astype(jnp.bfloat16)
    for copy in loads[1:]:
        copy.wait()
    slot_block = lax.broadcasted_iota(jnp.int32, (1, slots), 1) // ROW_BLOCK
    for point in range(points):
        live = slot_block < blocks[0:1, point : point + 1]
        widened = jnp.where(live, estimate[point].astype(jnp.float32), 0.0)
        masked = widened.astype(jnp.bfloat16)
        fetches[point].wait()
        product = jnp.dot(masked, pilots[point], preferred_element_type=jnp.float32)
        resid = received[point] - product + onsager[0:1, point : point + 1] * previous[point]
        resid_out[point] = resid
        square = jnp.sum(jnp.sum(resid * resid, axis=0, keepdims=True), axis=1, keepdims=True)
        spread = square / (antennas * resid.shape[1]) + epsilon
        narrow = resid.astype(jnp.bfloat16)
        stat = widened + lax.dot_general(
            narrow, pilots[point], (((1,), (1,)), ((), ())), preferred_element_type=jnp.float32
        )
        energy = jnp.sum(stat * stat, axis=0, keepdims=True)
        base = 0.5 * antennas * jnp.log(spread / (1.0 + spread))
        llr = jnp.where(live, base + energy / (2.0 * spread * (1.0 + spread)), 0.0)
        scaled[point] = jnp.where(live, stat / (1.0 + spread), 0.0)
        high, low = halves(llr)
        lanes = one_hot(lane_id[point : point + 1], LANES)
        values = jnp.concatenate(
            [
                jnp.where(lanes, high.astype(jnp.float32), 0.0).astype(jnp.bfloat16),
                jnp.where(lanes, low.astype(jnp.float32), 0.0).astype(jnp.bfloat16),
            ],
            axis=0,
        )
        for start in range(0, 2 * half_rows, TILE):
            both = lax.dot_general(
                selector[pl.ds(start, TILE), pl.ds(point * slots, slots)], values,
                (((1,), (1,)), ((), ())), preferred_element_type=jnp.float32,
            )
            term = both[:, :LANES] + both[:, LANES:]
            if point == 0:
                window[pl.ds(start, TILE), :] = term
            else:
                window[pl.ds(start, TILE), :] += term

    pl.semaphore_wait(barrier, peers)

    def swap(source, target, i):
        return pltpu.make_async_remote_copy(
            src_ref=source, dst_ref=target, send_sem=swap_sem.at[2 * i],
            recv_sem=swap_sem.at[2 * i + 1], device_id=partner, device_id_type=MESH,
        )

    first = swap(side(window, 1 - core), swapped, 0)
    first.start()
    stores = [
        pltpu.make_async_copy(resid_out, resid_hbm, store_sem.at[0]),
        pltpu.make_async_copy(scaled, scaled_hbm, store_sem.at[1]),
    ]
    for copy in stores:
        copy.start()
    total = jnp.zeros(owned.shape, jnp.float32)
    for k in range(prior.shape[1]):
        total = total + jnp.where(labels[...] == k, prior[0:1, k : k + 1], 0.0)
    first.wait_recv()
    half[...] = side(window, core)[...] + swapped[...]

    def sum_copy(source, target, device):
        return pltpu.make_async_remote_copy(
            src_ref=part(half, source), dst_ref=part(arrived, target),
            send_sem=sum_send.at[source], recv_sem=sum_recv.at[target],
            device_id=device, device_id_type=MESH,
        )

    def post_copy(source, target, device):
        return pltpu.make_async_remote_copy(
            src_ref=owned, dst_ref=part(nearby, core * peers + target),
            send_sem=post_send.at[source], recv_sem=post_recv.at[target],
            device_id=device, device_id_type=MESH,
        )

    @pl.loop(1, peers)
    def _(j):
        slot, back, device = peer(j)
        sum_copy(slot, back, device).start()

    total = total + part(half, home)[...]

    def collect(j, total):
        slot, _, device = peer(j)
        sum_copy(slot, slot, device).wait_recv()
        return total + part(arrived, slot)[...]

    posterior = jax.nn.sigmoid(lax.fori_loop(1, peers, collect, total))
    owned[...] = posterior

    @pl.loop(1, peers)
    def _(j):
        slot, back, device = peer(j)
        post_copy(slot, back, device).start()

    part(nearby, core * peers + home)[...] = posterior

    @pl.loop(1, peers)
    def _(j):
        slot, _, device = peer(j)
        post_copy(slot, slot, device).wait_recv()

    last = swap(side(nearby, core), side(nearby, core), 1)
    last.start()
    waiting = pltpu.make_async_remote_copy(
        src_ref=side(nearby, core), dst_ref=side(nearby, 1 - core), send_sem=swap_sem.at[2],
        recv_sem=swap_sem.at[3], device_id=partner, device_id_type=MESH,
    )
    waiting.wait_recv()
    finish = pltpu.make_async_copy(nearby, nearby_hbm, store_sem.at[2])
    finish.start()

    @pl.loop(1, peers)
    def _(j):
        slot, back, device = peer(j)
        sum_copy(slot, back, device).wait_send()
        post_copy(slot, back, device).wait_send()

    first.wait_send()
    last.wait_send()
    for copy in stores:
        copy.wait()
    finish.wait()


def denoise_kernel(
    users, visible_hbm, scaled_hbm, nearby_hbm, resid_hbm, fresh_hbm, resid_out, owned_out,
    visible, scaled, nearby, fresh, sem, store_sem,
):
    clusters, cluster = lax.axis_size("cluster"), lax.axis_index("cluster")
    rows = owned_out.shape[0]
    points = visible.shape[0]
    place = lax.rem(cluster, 2) * (3 * clusters // 2) + clusters // 2 + lax.div(cluster, 2)
    own_rows = pl.ds(pl.multiple_of(place * rows, rows), rows)
    copies = [
        pltpu.make_async_copy(source, target, sem.at[i])
        for i, (source, target) in enumerate(
            [
                (visible_hbm, visible), (nearby_hbm, nearby), (scaled_hbm, scaled),
                (resid_hbm, resid_out), (nearby_hbm.at[own_rows, :], owned_out),
            ]
        )
    ]
    for copy in copies:
        copy.start()
    copies[0].wait()
    row_id, lane_id = window_places(visible[...], users, rows)
    copies[1].wait()
    table = jnp.concatenate(halves(nearby[...]), axis=1)
    copies[2].wait()
    stores = []
    for point in range(points):
        picked = None
        for start in range(0, nearby.shape[0], TILE):
            hot = jnp.where(one_hot(row_id[point : point + 1], TILE, start), 1.0, 0.0)
            term = lax.dot_general(
                table[start : start + TILE], hot.astype(jnp.bfloat16), (((0,), (0,)), ((), ())),
                preferred_element_type=jnp.float32,
            )
            picked = term if picked is None else picked + term
        picked = picked[:LANES] + picked[LANES:]
        lanes = one_hot(lane_id[point : point + 1], LANES)
        rate = jnp.sum(jnp.where(lanes, picked, 0.0), axis=0, keepdims=True)
        fresh[point] = (rate * scaled[point]).astype(jnp.bfloat16)
        stores.append(
            pltpu.make_async_copy(fresh.at[point], fresh_hbm.at[point], store_sem.at[point])
        )
        stores[-1].start()
    for copy in copies[3:] + stores:
        copy.wait()


def local(
    pilots, estimate, visible, blocks, received, previous, onsager, user_cluster, cluster_prior
):
    points, antennas, slots = estimate.shape
    length = pilots.shape[2]
    users = user_cluster.shape[0]
    regions, clusters = lax.axis_size("region"), lax.axis_size("cluster")
    rows = users // (regions * clusters) // LANES
    peers = 3 * clusters // 2
    half_rows = peers * rows
    f32, i32, bf16 = jnp.float32, jnp.int32, jnp.bfloat16
    place = pl.BlockSpec(memory_space=pl.ANY)
    shape, vmem, dma = jax.ShapeDtypeStruct, pltpu.VMEM, pltpu.SemaphoreType.DMA
    resid, scaled, nearby = pl.pallas_call(
        main_kernel,
        in_specs=[place] * 9,
        out_specs=[place] * 3,
        out_shape=[
            shape((points, antennas, length), f32),
            shape((points, antennas, slots), f32),
            shape((2 * half_rows, LANES), f32),
        ],
        scratch_shapes=[
            vmem((points, slots, length), bf16),
            vmem((points, antennas, slots), bf16),
            vmem((points, slots), i32),
            vmem((1, points), i32),
            vmem((points, antennas, length), f32),
            vmem((points, antennas, length), f32),
            vmem((1, points), f32),
            vmem((rows, LANES), i32),
            vmem((1, cluster_prior.shape[0]), f32),
            vmem((points, antennas, length), f32),
            vmem((points, antennas, slots), f32),
            vmem((2 * half_rows, LANES), f32),
            vmem((2 * half_rows, points * slots), bf16),
            vmem((2 * half_rows, LANES), f32),
            vmem((half_rows, LANES), f32),
            vmem((half_rows, LANES), f32),
            vmem((half_rows, LANES), f32),
            vmem((rows, LANES), f32),
            dma((8,)), dma((points,)), dma((3,)), dma((4,)),
            dma((peers,)), dma((peers,)), dma((peers,)), dma((peers,)),
        ],
        compiler_params=pltpu.CompilerParams(
            collective_id=0, has_side_effects=True, vmem_limit_bytes=VMEM_LIMIT
        ),
    )(
        pilots, estimate, visible, blocks.reshape(1, -1), received, previous,
        onsager.reshape(1, -1), user_cluster.reshape(-1, LANES), cluster_prior.reshape(1, -1),
    )
    new_estimate, resid, owned = pl.pallas_call(
        functools.partial(denoise_kernel, users),
        in_specs=[place] * 4,
        out_specs=[place] * 3,
        out_shape=[
            shape((points, antennas, slots), bf16),
            shape((points, antennas, length), f32),
            shape((rows, LANES), f32),
        ],
        scratch_shapes=[
            vmem((points, slots), i32),
            vmem((points, antennas, slots), f32),
            vmem((2 * half_rows, LANES), f32),
            vmem((points, antennas, slots), bf16),
            dma((5,)), dma((points,)),
        ],
        compiler_params=pltpu.CompilerParams(vmem_limit_bytes=VMEM_LIMIT),
    )(visible, scaled, nearby, resid)
    return (new_estimate, resid, owned.reshape(-1))


def solution(mesh):
    device = ("region", "cluster")
    placed = (
        P(device, None, None),
        P(device, None, None),
        P(device, None),
        P(device),
        P(device, None, None),
        P(device, None, None),
        P(device),
        P(),
        P(),
    )
    return jax.shard_map(
        local,
        mesh=mesh,
        in_specs=placed,
        out_specs=(P(device, None, None), P(device, None, None), P(device)),
        check_vma=False,
    )
```

```python
import jax
import jax.numpy as jnp
from jax import lax
from jax.experimental import pallas as pl
from jax.experimental.pallas import tpu as pltpu
from jax.sharding import PartitionSpec as P

ROW_BLOCK = 128
LANES = 128
TILE = 384
VMEM_LIMIT = 48 * 1024 * 1024
MESH = pl.DeviceIdType.MESH

epsilon = 1e-06


def halves(value):
    high = value.astype(jnp.bfloat16)
    low = (value - high.astype(jnp.float32)).astype(jnp.bfloat16)
    return high, low


def window_places(visible, users, rows):
    regions, clusters = lax.axis_size("region"), lax.axis_size("cluster")
    lowest = lax.rem(lax.axis_index("region") + (regions - 1), regions) * (users // regions)
    shifted = visible - lowest
    shifted = jnp.where(shifted < 0, shifted + users, shifted)
    line = lax.div(shifted, LANES)
    device = lax.div(line, rows)
    place = lax.rem(device, 2) * (3 * clusters // 2) + lax.div(device, 2)
    return place * rows + lax.rem(line, rows), lax.rem(shifted, LANES)


def one_hot(row, count, start=0):
    place = lax.broadcasted_iota(jnp.int32, (count, row.shape[1]), 0) + start
    return place == row


def main_kernel(
    pilots_hbm, estimate_hbm, visible_hbm, blocks_hbm, received_hbm, previous_hbm, onsager_hbm,
    labels_hbm, prior_hbm,
    fresh_out, resid_out, owned_out,
    pilots, estimate, visible, blocks, received, previous, onsager, labels, prior,
    scaled, nearby, selector, window, swapped, half, arrived, owned,
    load_sem, pilot_sem, swap_sem, sum_send, sum_recv, post_send, post_recv,
):
    regions, clusters = lax.axis_size("region"), lax.axis_size("cluster")
    region, cluster = lax.axis_index("region"), lax.axis_index("cluster")
    core, chip, chips = lax.rem(cluster, 2), lax.div(cluster, 2), clusters // 2
    points, antennas, slots = estimate.shape
    rows = owned.shape[0]
    users = labels_hbm.shape[0] * LANES
    peers = 3 * chips
    half_rows = peers * rows
    home = chips + chip
    partner = (region, cluster + 1 - 2 * core)

    def part(ref, slot):
        return ref.at[pl.ds(pl.multiple_of(slot * rows, rows), rows), :]

    def side(ref, which):
        return ref.at[pl.ds(pl.multiple_of(which * half_rows, half_rows), half_rows), :]

    own_rows = pl.ds(pl.multiple_of((region * clusters + cluster) * rows, rows), rows)
    loads = [
        pltpu.make_async_copy(source, target, load_sem.at[i])
        for i, (source, target) in enumerate(
            [
                (visible_hbm, visible), (blocks_hbm, blocks), (estimate_hbm, estimate),
                (onsager_hbm, onsager), (received_hbm, received), (previous_hbm, previous),
                (prior_hbm, prior), (labels_hbm.at[own_rows, :], labels),
            ]
        )
    ]
    fetches = [
        pltpu.make_async_copy(pilots_hbm.at[i], pilots.at[i], pilot_sem.at[i])
        for i in range(points)
    ]
    for copy in loads[:4]:
        copy.start()
    fetches[0].start()
    for copy in loads[4:]:
        copy.start()
    for copy in fetches[1:]:
        copy.start()

    def peer(j):
        slot = lax.rem(home + j, peers)
        step = slot // chips
        device = (
            lax.rem(region + step + (regions - 1), regions), lax.rem(slot, chips) * 2 + core
        )
        back = (2 - step) * chips + chip
        return slot, back, device

    barrier = pltpu.get_barrier_semaphore()
    pl.semaphore_signal(barrier, inc=1, device_id=partner, device_id_type=MESH)

    @pl.loop(1, peers)
    def _(j):
        _, _, device = peer(j)
        pl.semaphore_signal(barrier, inc=1, device_id=device, device_id_type=MESH)

    loads[0].wait()
    row_id, lane_id = window_places(visible[...], users, rows)
    for copy in loads[1:]:
        copy.wait()
    slot_block = lax.broadcasted_iota(jnp.int32, (1, slots), 1) // ROW_BLOCK
    first_pass = []
    for point in range(points):
        live = slot_block < blocks[0:1, point : point + 1]
        widened = jnp.where(live, estimate[point].astype(jnp.float32), 0.0)
        masked = widened.astype(jnp.bfloat16)
        onward = received[point] + onsager[0:1, point : point + 1] * previous[point]
        fetches[point].wait()
        product = jnp.dot(masked, pilots[point], preferred_element_type=jnp.float32)
        for start in range(0, 2 * half_rows, TILE):
            selector[pl.ds(start, TILE), pl.ds(point * slots, slots)] = jnp.where(
                one_hot(row_id[point : point + 1], TILE, start), 1.0, 0.0
            ).astype(jnp.bfloat16)
        resid = onward - product
        resid_out[point] = resid
        square = jnp.sum(jnp.sum(resid * resid, axis=0, keepdims=True), axis=1, keepdims=True)
        spread = square / (antennas * resid.shape[1]) + epsilon
        first_pass.append((live, widened, resid.astype(jnp.bfloat16), spread))
    for point, (live, widened, narrow, spread) in enumerate(first_pass):
        stat = widened + lax.dot_general(
            narrow, pilots[point], (((1,), (1,)), ((), ())), preferred_element_type=jnp.float32
        )
        energy = jnp.sum(stat * stat, axis=0, keepdims=True)
        base = 0.5 * antennas * jnp.log(spread / (1.0 + spread))
        llr = jnp.where(live, base + energy / (2.0 * spread * (1.0 + spread)), 0.0)
        scaled[point] = jnp.where(live, stat / (1.0 + spread), 0.0)
        high, low = halves(llr)
        lanes = one_hot(lane_id[point : point + 1], LANES)
        values = jnp.concatenate(
            [
                jnp.where(lanes, high.astype(jnp.float32), 0.0).astype(jnp.bfloat16),
                jnp.where(lanes, low.astype(jnp.float32), 0.0).astype(jnp.bfloat16),
            ],
            axis=0,
        )
        for start in range(0, 2 * half_rows, TILE):
            both = lax.dot_general(
                selector[pl.ds(start, TILE), pl.ds(point * slots, slots)], values,
                (((1,), (1,)), ((), ())), preferred_element_type=jnp.float32,
            )
            term = both[:, :LANES] + both[:, LANES:]
            if point == 0:
                window[pl.ds(start, TILE), :] = term
            else:
                window[pl.ds(start, TILE), :] += term

    pl.semaphore_wait(barrier, peers)

    def swap(source, target, i):
        return pltpu.make_async_remote_copy(
            src_ref=source, dst_ref=target, send_sem=swap_sem.at[2 * i],
            recv_sem=swap_sem.at[2 * i + 1], device_id=partner, device_id_type=MESH,
        )

    first = swap(side(window, 1 - core), swapped, 0)
    first.start()
    total = jnp.zeros(owned.shape, jnp.float32)
    for k in range(prior.shape[1]):
        total = total + jnp.where(labels[...] == k, prior[0:1, k : k + 1], 0.0)
    first.wait_recv()
    half[...] = side(window, core)[...] + swapped[...]

    def sum_copy(source, target, device):
        return pltpu.make_async_remote_copy(
            src_ref=part(half, source), dst_ref=part(arrived, target),
            send_sem=sum_send.at[source], recv_sem=sum_recv.at[target],
            device_id=device, device_id_type=MESH,
        )

    def post_copy(source, target, device):
        return pltpu.make_async_remote_copy(
            src_ref=owned, dst_ref=part(nearby, core * peers + target),
            send_sem=post_send.at[source], recv_sem=post_recv.at[target],
            device_id=device, device_id_type=MESH,
        )

    @pl.loop(1, peers)
    def _(j):
        slot, back, device = peer(j)
        sum_copy(slot, back, device).start()

    total = total + part(half, home)[...]

    def collect(j, total):
        slot, _, device = peer(j)
        sum_copy(slot, slot, device).wait_recv()
        return total + part(arrived, slot)[...]

    posterior = jax.nn.sigmoid(lax.fori_loop(1, peers, collect, total))
    owned[...] = posterior
    owned_out[...] = posterior

    @pl.loop(1, peers)
    def _(j):
        slot, back, device = peer(j)
        post_copy(slot, back, device).start()

    part(nearby, core * peers + home)[...] = posterior

    @pl.loop(1, peers)
    def _(j):
        slot, _, device = peer(j)
        post_copy(slot, slot, device).wait_recv()

    last = swap(side(nearby, core), side(nearby, core), 1)
    last.start()
    waiting = pltpu.make_async_remote_copy(
        src_ref=side(nearby, core), dst_ref=side(nearby, 1 - core), send_sem=swap_sem.at[2],
        recv_sem=swap_sem.at[3], device_id=partner, device_id_type=MESH,
    )
    waiting.wait_recv()
    table = jnp.concatenate(halves(nearby[...]), axis=1)
    for point in range(points):
        picked = None
        for start in range(0, 2 * half_rows, TILE):
            term = lax.dot_general(
                table[start : start + TILE],
                selector[pl.ds(start, TILE), pl.ds(point * slots, slots)],
                (((0,), (0,)), ((), ())), preferred_element_type=jnp.float32,
            )
            picked = term if picked is None else picked + term
        picked = picked[:LANES] + picked[LANES:]
        lanes = one_hot(lane_id[point : point + 1], LANES)
        rate = jnp.sum(jnp.where(lanes, picked, 0.0), axis=0, keepdims=True)
        fresh_out[point] = (rate * scaled[point]).astype(jnp.bfloat16)

    @pl.loop(1, peers)
    def _(j):
        slot, back, device = peer(j)
        sum_copy(slot, back, device).wait_send()
        post_copy(slot, back, device).wait_send()

    first.wait_send()
    last.wait_send()


def store_kernel(fresh, resid, owned, fresh_hbm, resid_hbm, owned_hbm, sem):
    copies = [
        pltpu.make_async_copy(resid, resid_hbm, sem.at[0]),
        pltpu.make_async_copy(fresh, fresh_hbm, sem.at[1]),
        pltpu.make_async_copy(owned, owned_hbm, sem.at[2]),
    ]
    for copy in copies:
        copy.start()
    for copy in copies:
        copy.wait()


def local(
    pilots, estimate, visible, blocks, received, previous, onsager, user_cluster, cluster_prior
):
    points, antennas, slots = estimate.shape
    length = pilots.shape[2]
    users = user_cluster.shape[0]
    regions, clusters = lax.axis_size("region"), lax.axis_size("cluster")
    rows = users // (regions * clusters) // LANES
    peers = 3 * clusters // 2
    half_rows = peers * rows
    f32, i32, bf16 = jnp.float32, jnp.int32, jnp.bfloat16
    kept = pl.BlockSpec(memory_space=pltpu.HBM)
    near = pl.BlockSpec(memory_space=pltpu.VMEM)
    vmem, dma = pltpu.VMEM, pltpu.SemaphoreType.DMA
    results = [
        ((points, antennas, slots), bf16),
        ((points, antennas, length), f32),
        ((rows, LANES), f32),
    ]
    made = pl.pallas_call(
        main_kernel,
        in_specs=[kept] * 9,
        out_specs=[near] * 3,
        out_shape=[pltpu.VMEM(*result) for result in results],
        scratch_shapes=[
            vmem((points, slots, length), bf16),
            vmem((points, antennas, slots), bf16),
            vmem((points, slots), i32),
            vmem((1, points), i32),
            vmem((points, antennas, length), f32),
            vmem((points, antennas, length), f32),
            vmem((1, points), f32),
            vmem((rows, LANES), i32),
            vmem((1, cluster_prior.shape[0]), f32),
            vmem((points, antennas, slots), f32),
            vmem((2 * half_rows, LANES), f32),
            vmem((2 * half_rows, points * slots), bf16),
            vmem((2 * half_rows, LANES), f32),
            vmem((half_rows, LANES), f32),
            vmem((half_rows, LANES), f32),
            vmem((half_rows, LANES), f32),
            vmem((rows, LANES), f32),
            dma((8,)), dma((points,)), dma((4,)),
            dma((peers,)), dma((peers,)), dma((peers,)), dma((peers,)),
        ],
        compiler_params=pltpu.CompilerParams(
            collective_id=0, has_side_effects=True, vmem_limit_bytes=VMEM_LIMIT
        ),
    )(
        *[
            pltpu.with_memory_space_constraint(operand, pltpu.HBM)
            for operand in (
                pilots, estimate, visible, blocks.reshape(1, -1), received, previous,
                onsager.reshape(1, -1), user_cluster.reshape(-1, LANES),
                cluster_prior.reshape(1, -1),
            )
        ]
    )
    new_estimate, resid, owned = pl.pallas_call(
        store_kernel,
        in_specs=[near] * 3,
        out_specs=[kept] * 3,
        out_shape=[pltpu.HBM(*result) for result in results],
        scratch_shapes=[dma((3,))],
    )(*[pltpu.with_memory_space_constraint(result, pltpu.VMEM) for result in made])
    return (new_estimate, resid, owned.reshape(-1))


def solution(mesh):
    device = ("region", "cluster")
    placed = (
        P(device, None, None),
        P(device, None, None),
        P(device, None),
        P(device),
        P(device, None, None),
        P(device, None, None),
        P(device),
        P(),
        P(),
    )
    return jax.shard_map(
        local,
        mesh=mesh,
        in_specs=placed,
        out_specs=(P(device, None, None), P(device, None, None), P(device)),
        check_vma=False,
    )
```

```python
import jax
import jax.numpy as jnp
from jax import lax
from jax.experimental import pallas as pl
from jax.experimental.pallas import tpu as pltpu
from jax.sharding import PartitionSpec as P

ROW_BLOCK = 128
LANES = 128
TILE = 384
VMEM_LIMIT = 48 * 1024 * 1024
MESH = pl.DeviceIdType.MESH

epsilon = 1e-06


def halves(value):
    high = value.astype(jnp.bfloat16)
    low = (value - high.astype(jnp.float32)).astype(jnp.bfloat16)
    return high, low


def window_places(visible, users, rows):
    regions, clusters = lax.axis_size("region"), lax.axis_size("cluster")
    lowest = lax.rem(lax.axis_index("region") + (regions - 1), regions) * (users // regions)
    shifted = visible - lowest
    shifted = jnp.where(shifted < 0, shifted + users, shifted)
    line = lax.div(shifted, LANES)
    device = lax.div(line, rows)
    place = lax.rem(device, 2) * (3 * clusters // 2) + lax.div(device, 2)
    return place * rows + lax.rem(line, rows), lax.rem(shifted, LANES)


def one_hot(row, count, start=0):
    place = lax.broadcasted_iota(jnp.int32, (count, row.shape[1]), 0) + start
    return place == row


def main_kernel(
    pilots_hbm, estimate_hbm, visible_hbm, blocks_hbm, received_hbm, previous_hbm, onsager_hbm,
    labels_hbm, prior_hbm,
    fresh_out, resid_out, owned_out,
    pilots, estimate, visible, blocks, received, previous, onsager, labels, prior,
    scaled, nearby, selector, window, swapped, half, arrived, owned,
    load_sem, pilot_sem, swap_sem, sum_send, sum_recv, post_send, post_recv,
):
    regions, clusters = lax.axis_size("region"), lax.axis_size("cluster")
    region, cluster = lax.axis_index("region"), lax.axis_index("cluster")
    core, chip, chips = lax.rem(cluster, 2), lax.div(cluster, 2), clusters // 2
    points, antennas, slots = estimate.shape
    rows = owned.shape[0]
    users = labels_hbm.shape[0] * LANES
    peers = 3 * chips
    half_rows = peers * rows
    home = chips + chip
    partner = (region, cluster + 1 - 2 * core)

    def part(ref, slot):
        return ref.at[pl.ds(pl.multiple_of(slot * rows, rows), rows), :]

    def side(ref, which):
        return ref.at[pl.ds(pl.multiple_of(which * half_rows, half_rows), half_rows), :]

    own_rows = pl.ds(pl.multiple_of((region * clusters + cluster) * rows, rows), rows)
    loads = [
        pltpu.make_async_copy(source, target, load_sem.at[i])
        for i, (source, target) in enumerate(
            [
                (visible_hbm, visible), (blocks_hbm, blocks), (estimate_hbm, estimate),
                (onsager_hbm, onsager), (received_hbm, received), (previous_hbm, previous),
                (prior_hbm, prior), (labels_hbm.at[own_rows, :], labels),
            ]
        )
    ]
    fetches = [
        pltpu.make_async_copy(pilots_hbm.at[i], pilots.at[i], pilot_sem.at[i])
        for i in range(points)
    ]
    for copy in loads[:4]:
        copy.start()
    fetches[0].start()
    for copy in loads[4:]:
        copy.start()
    for copy in fetches[1:]:
        copy.start()

    def peer(j):
        slot = lax.rem(home + j, peers)
        step = slot // chips
        device = (
            lax.rem(region + step + (regions - 1), regions), lax.rem(slot, chips) * 2 + core
        )
        back = (2 - step) * chips + chip
        return slot, back, device

    barrier = pltpu.get_barrier_semaphore()
    pl.semaphore_signal(barrier, inc=1, device_id=partner, device_id_type=MESH)

    @pl.loop(1, peers)
    def _(j):
        _, _, device = peer(j)
        pl.semaphore_signal(barrier, inc=1, device_id=device, device_id_type=MESH)

    loads[0].wait()
    row_id, lane_id = window_places(visible[...], users, rows)
    for copy in loads[1:]:
        copy.wait()
    slot_block = lax.broadcasted_iota(jnp.int32, (1, slots), 1) // ROW_BLOCK
    first_pass = []
    for point in range(points):
        live = slot_block < blocks[0:1, point : point + 1]
        widened = jnp.where(live, estimate[point].astype(jnp.float32), 0.0)
        masked = widened.astype(jnp.bfloat16)
        onward = received[point] + onsager[0:1, point : point + 1] * previous[point]
        fetches[point].wait()
        product = jnp.dot(masked, pilots[point], preferred_element_type=jnp.float32)
        for start in range(0, 2 * half_rows, TILE):
            selector[pl.ds(start, TILE), pl.ds(point * slots, slots)] = jnp.where(
                one_hot(row_id[point : point + 1], TILE, start), 1.0, 0.0
            ).astype(jnp.bfloat16)
        resid = onward - product
        resid_out[point] = resid
        square = jnp.sum(jnp.sum(resid * resid, axis=0, keepdims=True), axis=1, keepdims=True)
        spread = square / (antennas * resid.shape[1]) + epsilon
        first_pass.append((live, widened, resid.astype(jnp.bfloat16), spread))
    for point, (live, widened, narrow, spread) in enumerate(first_pass):
        stat = widened + lax.dot_general(
            narrow, pilots[point], (((1,), (1,)), ((), ())), preferred_element_type=jnp.float32
        )
        energy = jnp.sum(stat * stat, axis=0, keepdims=True)
        base = 0.5 * antennas * jnp.log(spread / (1.0 + spread))
        llr = jnp.where(live, base + energy / (2.0 * spread * (1.0 + spread)), 0.0)
        scaled[point] = jnp.where(live, stat / (1.0 + spread), 0.0)
        high, low = halves(llr)
        lanes = one_hot(lane_id[point : point + 1], LANES)
        values = jnp.concatenate(
            [
                jnp.where(lanes, high.astype(jnp.float32), 0.0).astype(jnp.bfloat16),
                jnp.where(lanes, low.astype(jnp.float32), 0.0).astype(jnp.bfloat16),
            ],
            axis=0,
        )
        for start in range(0, 2 * half_rows, TILE):
            both = lax.dot_general(
                selector[pl.ds(start, TILE), pl.ds(point * slots, slots)], values,
                (((1,), (1,)), ((), ())), preferred_element_type=jnp.float32,
            )
            term = both[:, :LANES] + both[:, LANES:]
            if point == 0:
                window[pl.ds(start, TILE), :] = term
            else:
                window[pl.ds(start, TILE), :] += term

    pl.semaphore_wait(barrier, peers)

    def swap(source, target, i):
        return pltpu.make_async_remote_copy(
            src_ref=source, dst_ref=target, send_sem=swap_sem.at[2 * i],
            recv_sem=swap_sem.at[2 * i + 1], device_id=partner, device_id_type=MESH,
        )

    first = swap(side(window, 1 - core), swapped, 0)
    first.start()
    total = jnp.zeros(owned.shape, jnp.float32)
    for k in range(prior.shape[1]):
        total = total + jnp.where(labels[...] == k, prior[0:1, k : k + 1], 0.0)
    first.wait_recv()
    half[...] = side(window, core)[...] + swapped[...]

    def sum_copy(source, target, device):
        return pltpu.make_async_remote_copy(
            src_ref=part(half, source), dst_ref=part(arrived, target),
            send_sem=sum_send.at[source], recv_sem=sum_recv.at[target],
            device_id=device, device_id_type=MESH,
        )

    def post_copy(source, target, device):
        return pltpu.make_async_remote_copy(
            src_ref=owned, dst_ref=part(nearby, core * peers + target),
            send_sem=post_send.at[source], recv_sem=post_recv.at[target],
            device_id=device, device_id_type=MESH,
        )

    @pl.loop(1, peers)
    def _(j):
        slot, back, device = peer(j)
        sum_copy(slot, back, device).start()

    total = total + part(half, home)[...]

    def collect(j, total):
        slot, _, device = peer(j)
        sum_copy(slot, slot, device).wait_recv()
        return total + part(arrived, slot)[...]

    posterior = jax.nn.sigmoid(lax.fori_loop(1, peers, collect, total))
    owned[...] = posterior
    owned_out[...] = posterior

    @pl.loop(1, peers)
    def _(j):
        slot, back, device = peer(j)
        post_copy(slot, back, device).start()

    part(nearby, core * peers + home)[...] = posterior

    @pl.loop(1, peers)
    def _(j):
        slot, _, device = peer(j)
        post_copy(slot, slot, device).wait_recv()

    last = swap(side(nearby, core), side(nearby, core), 1)
    last.start()
    waiting = pltpu.make_async_remote_copy(
        src_ref=side(nearby, core), dst_ref=side(nearby, 1 - core), send_sem=swap_sem.at[2],
        recv_sem=swap_sem.at[3], device_id=partner, device_id_type=MESH,
    )
    @pl.loop(1, peers)
    def _(j):
        slot, back, device = peer(j)
        sum_copy(slot, back, device).wait_send()
        post_copy(slot, back, device).wait_send()

    waiting.wait_recv()
    table = nearby[...].astype(jnp.bfloat16)
    for point in range(points):
        picked = None
        for start in range(0, 2 * half_rows, TILE):
            term = lax.dot_general(
                table[start : start + TILE],
                selector[pl.ds(start, TILE), pl.ds(point * slots, slots)],
                (((0,), (0,)), ((), ())), preferred_element_type=jnp.float32,
            )
            picked = term if picked is None else picked + term
        lanes = one_hot(lane_id[point : point + 1], LANES)
        rate = jnp.sum(jnp.where(lanes, picked, 0.0), axis=0, keepdims=True)
        fresh_out[point] = (rate * scaled[point]).astype(jnp.bfloat16)

    first.wait_send()
    last.wait_send()


def store_kernel(fresh, resid, owned, fresh_hbm, resid_hbm, owned_hbm, sem):
    copies = [
        pltpu.make_async_copy(resid, resid_hbm, sem.at[0]),
        pltpu.make_async_copy(fresh, fresh_hbm, sem.at[1]),
        pltpu.make_async_copy(owned, owned_hbm, sem.at[2]),
    ]
    for copy in copies:
        copy.start()
    for copy in copies:
        copy.wait()


def local(
    pilots, estimate, visible, blocks, received, previous, onsager, user_cluster, cluster_prior
):
    points, antennas, slots = estimate.shape
    length = pilots.shape[2]
    users = user_cluster.shape[0]
    regions, clusters = lax.axis_size("region"), lax.axis_size("cluster")
    rows = users // (regions * clusters) // LANES
    peers = 3 * clusters // 2
    half_rows = peers * rows
    f32, i32, bf16 = jnp.float32, jnp.int32, jnp.bfloat16
    kept = pl.BlockSpec(memory_space=pltpu.HBM)
    near = pl.BlockSpec(memory_space=pltpu.VMEM)
    vmem, dma = pltpu.VMEM, pltpu.SemaphoreType.DMA
    results = [
        ((points, antennas, slots), bf16),
        ((points, antennas, length), f32),
        ((rows, LANES), f32),
    ]
    made = pl.pallas_call(
        main_kernel,
        in_specs=[kept] * 9,
        out_specs=[near] * 3,
        out_shape=[pltpu.VMEM(*result) for result in results],
        scratch_shapes=[
            vmem((points, slots, length), bf16),
            vmem((points, antennas, slots), bf16),
            vmem((points, slots), i32),
            vmem((1, points), i32),
            vmem((points, antennas, length), f32),
            vmem((points, antennas, length), f32),
            vmem((1, points), f32),
            vmem((rows, LANES), i32),
            vmem((1, cluster_prior.shape[0]), f32),
            vmem((points, antennas, slots), f32),
            vmem((2 * half_rows, LANES), f32),
            vmem((2 * half_rows, points * slots), bf16),
            vmem((2 * half_rows, LANES), f32),
            vmem((half_rows, LANES), f32),
            vmem((half_rows, LANES), f32),
            vmem((half_rows, LANES), f32),
            vmem((rows, LANES), f32),
            dma((8,)), dma((points,)), dma((4,)),
            dma((peers,)), dma((peers,)), dma((peers,)), dma((peers,)),
        ],
        compiler_params=pltpu.CompilerParams(
            collective_id=0, has_side_effects=True, vmem_limit_bytes=VMEM_LIMIT
        ),
    )(
        *[
            pltpu.with_memory_space_constraint(operand, pltpu.HBM)
            for operand in (
                pilots, estimate, visible, blocks.reshape(1, -1), received, previous,
                onsager.reshape(1, -1), user_cluster.reshape(-1, LANES),
                cluster_prior.reshape(1, -1),
            )
        ]
    )
    new_estimate, resid, owned = pl.pallas_call(
        store_kernel,
        in_specs=[near] * 3,
        out_specs=[kept] * 3,
        out_shape=[pltpu.HBM(*result) for result in results],
        scratch_shapes=[dma((3,))],
    )(*[pltpu.with_memory_space_constraint(result, pltpu.VMEM) for result in made])
    return (new_estimate, resid, owned.reshape(-1))


def solution(mesh):
    device = ("region", "cluster")
    placed = (
        P(device, None, None),
        P(device, None, None),
        P(device, None),
        P(device),
        P(device, None, None),
        P(device, None, None),
        P(device),
        P(),
        P(),
    )
    return jax.shard_map(
        local,
        mesh=mesh,
        in_specs=placed,
        out_specs=(P(device, None, None), P(device, None, None), P(device)),
        check_vma=False,
    )
```
